32 devices in a mesh: row: 4 (over z), col: 8 (over y, x, core).
Axes of the slice: x: 2, y: 2, z: 4, core: 2. Of those that a mesh axis runs over, the one named last changes fastest.
Arguments:
- table: float32 [32, 512, 512], P(None, 'row', 'col'), may hold values from -50 to 50
- in_weight: bfloat16 [2, 128, 128], replicated, may hold values from -0.5 to 0.5
- in_bias: float32 [2, 128], replicated, may hold values from -3 to 3
- mid_weight: bfloat16 [2, 128, 128], replicated, may hold values from -0.5 to 0.5
- mid_bias: float32 [2, 128], replicated, may hold values from -3 to 3
- out_weight: bfloat16 [2, 128, 32], replicated, may hold values from -0.5 to 0.5
- out_bias: float32 [2, 32], replicated, may hold values from -3 to 3
Outputs:
- out_table: float32 [32, 512, 512], P(None, 'row', 'col')
The draws below stay inside these ranges and needn't reach their ends.
All inputs are finite; a program needn't handle non-finite values.
Results may differ from the reference program's by a relative error of at most 0.0068.
Values may be sent and summed in bfloat16 or wider, within the bound.
A program may use at most 64 MiB of HBM per device.

```python
import math
import jax
import jax.numpy as jnp
from jax import lax

CHANNELS = 32
HIDDEN_UNITS = 128
LAYERS = 2
ENTITIES = 512
N_ROW = 4


def draw_table(key, part):
    keys = jax.random.split(jax.random.fold_in(key, 11), 3)
    ramp = jnp.arange(ENTITIES, dtype=jnp.float32) / max(ENTITIES - 1, 1)
    row_scale = jnp.power(3.0, ramp) * jnp.exp(jax.random.uniform(keys[1], (ENTITIES,), jnp.float32, -0.6, 0.6)) / 1.7
    col_scale = jnp.power(3.0, ramp) * jnp.exp(jax.random.uniform(keys[2], (ENTITIES,), jnp.float32, -0.6, 0.6)) / 1.7
    base = jnp.clip(jax.random.normal(keys[0], (CHANNELS, ENTITIES, ENTITIES), jnp.float32), -4.0, 4.0)
    return base * row_scale[None, :, None] * col_scale[None, None, :]


def centred(own_key, extent, spread, bound, held_as=jnp.bfloat16):
    drawn = spread * jax.random.normal(own_key, extent, jnp.float32)
    return jnp.clip(drawn, min=-bound, max=bound).astype(held_as)


def setup_inputs(seed: int = 0) -> dict:
    seeds = jax.random.split(jax.random.key(seed), 8)
    return {
        "table": draw_table(jax.random.fold_in(seeds[7], 71), 0),
        "in_weight": centred(seeds[1], (LAYERS, 4 * CHANNELS, HIDDEN_UNITS), (4 * CHANNELS) ** -0.5, 0.5),
        "in_bias": centred(seeds[2], (LAYERS, HIDDEN_UNITS), 0.5, 3.0, jnp.float32),
        "mid_weight": centred(seeds[3], (LAYERS, HIDDEN_UNITS, HIDDEN_UNITS), HIDDEN_UNITS ** -0.5, 0.5),
        "mid_bias": centred(seeds[4], (LAYERS, HIDDEN_UNITS), 0.5, 3.0, jnp.float32),
        "out_weight": centred(seeds[5], (LAYERS, HIDDEN_UNITS, CHANNELS), HIDDEN_UNITS ** -0.5, 0.5),
        "out_bias": centred(seeds[6], (LAYERS, CHANNELS), 0.5, 3.0, jnp.float32),
    }


def evaluate(own_part, pair_part, row_pool, col_pool, in_weight, in_bias, mid_weight, mid_bias, out_weight, out_bias, layer_idx):
    channels = own_part.shape[0]
    w_first = in_weight[layer_idx].astype(jnp.float32)
    w_own = w_first[:channels]
    w_pair = w_first[channels:2 * channels]
    w_row = w_first[2 * channels:3 * channels]
    w_col = w_first[3 * channels:]
    mid_mat = mid_weight[layer_idx].astype(jnp.float32)
    out_mat = out_weight[layer_idx].astype(jnp.float32)
    mid_shift = mid_bias[layer_idx]
    out_shift = out_bias[layer_idx]
    row_term = jnp.einsum('ck,cr->kr', w_row, row_pool.astype(jnp.bfloat16).astype(jnp.float32))
    col_term = jnp.einsum('ck,cj->kj', w_col, col_pool.astype(jnp.bfloat16).astype(jnp.float32)) + in_bias[layer_idx][:, None]
    row_count = own_part.shape[1]
    col_count = own_part.shape[2]
    block_rows = row_count // N_ROW
    result = jnp.zeros((out_mat.shape[1], row_count, col_count), jnp.float32)

    def fill_block(block_idx, result):
        row_start = (block_idx * block_rows).astype(jnp.int32)
        own_rows = lax.dynamic_slice_in_dim(own_part, row_start, block_rows, 1).astype(jnp.bfloat16).astype(jnp.float32)
        pair_rows = lax.dynamic_slice_in_dim(pair_part, row_start, block_rows, 1).astype(jnp.bfloat16).astype(jnp.float32)
        row_share = lax.dynamic_slice_in_dim(row_term, row_start, block_rows, 1)
        first_pre = jnp.einsum('ck,crj->krj', w_own, own_rows) + jnp.einsum('ck,crj->krj', w_pair, pair_rows)
        first_pre = first_pre + row_share[:, :, None] + col_term[:, None, :]
        hidden = jax.nn.relu(first_pre).astype(jnp.bfloat16).astype(jnp.float32)
        second = jnp.einsum('hk,hrj->krj', mid_mat, hidden) + mid_shift[:, None, None]
        second = jax.nn.relu(second).astype(jnp.bfloat16).astype(jnp.float32)
        final_out = jnp.einsum('kc,krj->crj', out_mat, second) + out_shift[:, None, None]
        return lax.dynamic_update_slice_in_dim(result, final_out, row_start, 1)
    return lax.fori_loop(0, N_ROW, fill_block, result)

def one_layer(values, in_weight, in_bias, mid_weight, mid_bias, out_weight, out_bias, layer_idx):
    pool_scale = 1.0 / math.sqrt(values.shape[1])
    row_pool = lax.optimization_barrier(jnp.sum(values, axis=2)) * pool_scale
    col_pool = lax.optimization_barrier(jnp.sum(values, axis=1)) * pool_scale
    pair_part = jnp.swapaxes(values, 1, 2).astype(jnp.bfloat16)
    return evaluate(values, pair_part, row_pool, col_pool, in_weight, in_bias, mid_weight, mid_bias, out_weight, out_bias, layer_idx)

def reference(table, in_weight, in_bias, mid_weight, mid_bias, out_weight, out_bias):
    first_out = one_layer(table, in_weight, in_bias, mid_weight, mid_bias, out_weight, out_bias, 0)
    return one_layer(first_out, in_weight, in_bias, mid_weight, mid_bias, out_weight, out_bias, 1)
```

```python
import functools
import math

import jax
import jax.numpy as jnp
from jax import lax
from jax.experimental import pallas as pl
from jax.experimental.pallas import tpu as pltpu
from jax.sharding import PartitionSpec as P

MESH = pl.DeviceIdType.MESH
BF = jnp.bfloat16
F32 = jnp.float32
LANES = 128


def dot(a, b):
    return jnp.dot(a, b, preferred_element_type=F32)


def kernel(
    dims,
    table,
    w_in,
    b_in,
    w_mid,
    b_mid,
    w_out,
    b_out,
    out,
    flat,
    turned,
    send,
    pair,
    own,
    own2,
    mir2,
    wt_in,
    wt_mid,
    bt_in,
    bt_mid,
    bt_out,
    spread,
    gather,
    col_chunks,
    row_part,
    col_part,
    row_recv,
    col_recv,
    mate_send,
    mate_recv,
    acc_row,
    acc_col,
    bulk_ssem,
    bulk_rsem,
    row_ssem,
    row_rsem,
    col_ssem,
    col_rsem,
    mate_ssem,
    mate_rsem,
):
    ch, tr, tc, n_row, n_col, q, nb, layers = dims
    pack = LANES // tc if tc < LANES else 1
    width = pack * tc
    bc = tc // nb
    lanes = bc * tr
    hid = w_mid.shape[1]
    scale = 1.0 / math.sqrt(tr * n_row)
    r = lax.axis_index("row")
    c = lax.axis_index("col")
    mir_r = c // q
    mir_c0 = q * r
    slot = c % q
    diag = mir_r == r

    barrier = pltpu.get_barrier_semaphore()
    for d in range(1, n_col):
        pl.semaphore_signal(
            barrier, inc=1, device_id=(r, lax.rem(c + d, n_col)), device_id_type=MESH
        )
    for d in range(1, n_row):
        pl.semaphore_signal(
            barrier, inc=1, device_id=(lax.rem(r + d, n_row), c), device_id_type=MESH
        )

    @pl.when(jnp.logical_not(diag))
    def _():
        for h in range(q):
            pl.semaphore_signal(
                barrier, inc=1, device_id=(mir_r, mir_c0 + h), device_id_type=MESH
            )

    groups = tr // LANES

    if groups > 1:
        for v in range(groups):
            flat[v * ch * tc : (v + 1) * ch * tc, :] = table[:, v * LANES : (v + 1) * LANES]

    def column_of(j):
        if groups == 1:
            return table[pl.ds(j, ch, stride=tc), :]
        parts = [flat[pl.ds(v * ch * tc + j, ch, stride=tc), :] for v in range(groups)]
        return jnp.concatenate(parts, axis=1)

    def turn_step(i, carry):
        src = pl.multiple_of(i * tc, tc)
        dst = pl.multiple_of(i * tr, tr)
        turned[pl.ds(dst, tr), :] = table[pl.ds(src, tc), :].T
        return carry

    lax.fori_loop(0, ch, turn_step, 0, unroll=4)

    def own_step(g, acc):
        for m in range(bc):
            val = column_of(g * bc + m)
            acc = acc + val
            own[g, :, m * tr : (m + 1) * tr] = val.astype(BF)
        return acc

    row_part[0] = lax.fori_loop(0, nb, own_step, jnp.zeros((ch, tr), F32))

    def col_step(i, acc):
        for u in range(8):
            acc = acc + turned[pl.ds(i * 8 + u, ch, stride=tr), :]
        return acc

    acc = lax.fori_loop(0, tr // 8, col_step, jnp.zeros((ch, tc), F32))
    col_part[0] = jnp.concatenate([acc] * pack, axis=1) if pack > 1 else acc

    @pl.when(diag)
    def _():
        pl.semaphore_wait(barrier, n_col - 1 + n_row - 1)

    @pl.when(jnp.logical_not(diag))
    def _():
        pl.semaphore_wait(barrier, n_col - 1 + n_row - 1 + q)

    def row_copy(layer, d):
        return pltpu.make_async_remote_copy(
            src_ref=row_part.at[layer],
            dst_ref=row_recv.at[layer, d - 1],
            send_sem=row_ssem.at[layer, d - 1],
            recv_sem=row_rsem.at[layer, d - 1],
            device_id=(r, lax.rem(c + d, n_col)),
            device_id_type=MESH,
        )

    def col_copy(layer, d):
        return pltpu.make_async_remote_copy(
            src_ref=col_part.at[layer],
            dst_ref=col_recv.at[layer, d - 1],
            send_sem=col_ssem.at[layer, d - 1],
            recv_sem=col_rsem.at[layer, d - 1],
            device_id=(lax.rem(r + d, n_row), c),
            device_id_type=MESH,
        )

    def pools_start(layer):
        for d in range(1, n_row):
            col_copy(layer, d).start()
        for d in range(1, n_col):
            row_copy(layer, d).start()

    def pools_finish(layer):
        row_sum = row_part[layer]
        col_sum = col_part[layer]
        for d in range(1, n_row):
            col_copy(layer, d).wait()
            col_sum = col_sum + col_recv[layer, d - 1]
        for d in range(1, n_col):
            row_copy(layer, d).wait()
            row_sum = row_sum + row_recv[layer, d - 1]
        return row_sum * scale, col_sum * scale

    pools_start(0)

    def bulk_copy(h, k):
        return pltpu.make_async_remote_copy(
            src_ref=send.at[h, k],
            dst_ref=pair.at[slot * nb + k],
            send_sem=bulk_ssem.at[h, k],
            recv_sem=bulk_rsem.at[slot * nb + k],
            device_id=(mir_r, mir_c0 + h),
            device_id_type=MESH,
        )

    def stay_copy(h, k):
        return pltpu.make_async_copy(
            send.at[h, k], pair.at[slot * nb + k], bulk_rsem.at[slot * nb + k]
        )

    for k in range(nb):
        for h in range(q):
            for m in range(bc // pack):
                base = h * tc + k * bc + m * pack
                parts = [turned[pl.ds(base + u, ch, stride=tr), :] for u in range(pack)]
                val = jnp.concatenate(parts, axis=1) if pack > 1 else parts[0]
                send[h, k, :, m * width : (m + 1) * width] = val.astype(BF)
        for h in range(q):
            here = jnp.logical_and(diag, slot == h)

            @pl.when(here)
            def _():
                stay_copy(h, k).start()

            @pl.when(jnp.logical_not(here))
            def _():
                bulk_copy(h, k).start()

    for layer in range(layers):
        wt_in[layer] = w_in[layer].astype(F32).T.astype(BF)
        wt_mid[layer] = w_mid[layer].astype(F32).T.astype(BF)
        bt_in[layer] = jnp.broadcast_to(b_in[layer : layer + 1, :], (LANES, hid)).T
        bt_mid[layer] = jnp.broadcast_to(b_mid[layer : layer + 1, :], (LANES, hid)).T
        bt_out[layer] = jnp.broadcast_to(b_out[layer : layer + 1, :], (LANES, ch)).T
    cell_col = lax.broadcasted_iota(jnp.int32, (bc, lanes), 1) // tr
    spread[...] = jnp.where(
        cell_col == lax.broadcasted_iota(jnp.int32, (bc, lanes), 0), 1.0, 0.0
    ).astype(BF)
    cell_col = lax.broadcasted_iota(jnp.int32, (lanes, width), 0) // tr
    gather[...] = jnp.where(
        cell_col == lax.broadcasted_iota(jnp.int32, (lanes, width), 1), 1.0, 0.0
    ).astype(BF)

    rp, cp = pools_finish(0)
    rp = rp.astype(BF)
    cp = cp.astype(BF)
    for h in range(q):
        half = rp[:, h * tc : (h + 1) * tc]
        half = jnp.concatenate([half] * pack, axis=1) if pack > 1 else half
        mate_send[h, :ch, :] = half
        mate_send[h, ch:, :] = cp

    def mate_copy(h):
        return pltpu.make_async_remote_copy(
            src_ref=mate_send.at[h],
            dst_ref=mate_recv.at[slot],
            send_sem=mate_ssem.at[h],
            recv_sem=mate_rsem.at[slot],
            device_id=(mir_r, mir_c0 + h),
            device_id_type=MESH,
        )

    def mate_stay(h):
        return pltpu.make_async_copy(mate_send.at[h], mate_recv.at[slot], mate_rsem.at[slot])

    for h in range(q):
        here = jnp.logical_and(diag, slot == h)

        @pl.when(here)
        def _():
            mate_stay(h).start()

        @pl.when(jnp.logical_not(here))
        def _():
            mate_copy(h).start()

    for t in range(q):
        pltpu.make_async_copy(mate_send.at[0], mate_recv.at[t], mate_rsem.at[t]).wait()
    cp_rows = jnp.concatenate([mate_recv[t, ch:, :tc] for t in range(q)], axis=1)
    rp_rows = rp
    for g in range(nb):
        col_chunks[g, :ch, :] = cp[:, g * bc : (g + 1) * bc]
        col_chunks[g, ch:, :] = mate_recv[0, :ch, g * bc : (g + 1) * bc]

    def tile(x):
        return jnp.concatenate([x] * (lanes // x.shape[1]), axis=1)

    def network(layer, feats):
        h1 = dot(wt_in[layer], feats) + tile(bt_in[layer])
        h1 = jnp.maximum(h1, 0.0).astype(BF)
        h2 = dot(wt_mid[layer], h1) + tile(bt_mid[layer])
        h2 = jnp.maximum(h2, 0.0).astype(BF)
        return dot(w_out[layer], h2) + tile(bt_out[layer])

    acc_row[...] = jnp.zeros_like(acc_row)
    acc_col[...] = jnp.zeros_like(acc_col)

    def layer_one(g, carry):
        for t in range(q):
            pltpu.make_async_copy(
                send.at[0, 0], pair.at[t * nb + g], bulk_rsem.at[t * nb + g]
            ).wait()
        mine = own[g]
        pieces = [
            pair[t * nb + g, :, a * tc : (a + 1) * tc] for a in range(bc) for t in range(q)
        ]
        theirs = jnp.concatenate(pieces, axis=1)
        wide = dot(col_chunks[g], spread[...]).astype(BF)
        straight = jnp.concatenate([mine, theirs, tile(rp_rows), wide[:ch]], axis=0)
        value = network(0, straight)
        top = value.astype(BF)
        own2[g] = top
        low = (value - top.astype(F32)).astype(BF)
        sums = dot(jnp.concatenate([top, low], axis=0), gather[...])
        sums = sums[:ch] + sums[ch:]
        acc_col[...] += pltpu.roll(sums, g * bc, 1)
        total = acc_row[...]
        for m in range(bc):
            total = total + value[:, m * tr : (m + 1) * tr]
        acc_row[...] = total
        mirrored = jnp.concatenate([theirs, mine, wide[ch:], tile(cp_rows)], axis=0)
        mir2[g] = network(0, mirrored).astype(BF)
        return carry

    lax.fori_loop(0, nb, layer_one, 0)
    row_part[1] = acc_row[...]
    col_part[1] = acc_col[...]
    pools_start(1)

    for k in range(nb):
        for h in range(q):
            here = jnp.logical_and(diag, slot == h)

            @pl.when(jnp.logical_not(here))
            def _():
                bulk_copy(h, k).wait_send()

    for h in range(q):
        here = jnp.logical_and(diag, slot == h)

        @pl.when(jnp.logical_not(here))
        def _():
            mate_copy(h).wait_send()

    rp, cp = pools_finish(1)
    rp_two = rp.astype(BF)
    cp = cp.astype(BF)
    for g in range(nb):
        col_chunks[g, :ch, :] = cp[:, g * bc : (g + 1) * bc]

    def layer_two(g, carry):
        wide = dot(col_chunks[g, :ch, :], spread[...]).astype(BF)
        feats = jnp.concatenate([own2[g], mir2[g], tile(rp_two), wide], axis=0)
        value = network(1, feats)
        for m in range(bc):
            for v in range(groups):
                at = m * tr + v * LANES
                rows = pl.ds(v * ch * tc + g * bc + m, ch, stride=tc)
                if groups == 1:
                    out[rows, :] = value[:, at : at + LANES]
                else:
                    flat[rows, :] = value[:, at : at + LANES]
        return carry

    lax.fori_loop(0, nb, layer_two, 0)
    if groups > 1:
        for v in range(groups):
            out[:, v * LANES : (v + 1) * LANES] = flat[v * ch * tc : (v + 1) * ch * tc, :]


def body(table, in_weight, in_bias, mid_weight, mid_bias, out_weight, out_bias):
    ch, tr, tc = table.shape
    n_row = lax.axis_size("row")
    n_col = lax.axis_size("col")
    layers, _, hid = in_weight.shape
    q = tr // tc
    assert tr == q * tc and n_col == q * n_row
    nb = 8
    pack = LANES // tc if tc < LANES else 1
    width = pack * tc
    bc = tc // nb
    lanes = bc * tr
    dims = (ch, tr, tc, n_row, n_col, q, nb, layers)
    dma = pltpu.SemaphoreType.DMA
    vmem = pl.BlockSpec(memory_space=pltpu.VMEM)
    result = pl.pallas_call(
        functools.partial(kernel, dims),
        out_shape=jax.ShapeDtypeStruct((ch * tc, tr), F32),
        in_specs=[vmem] * 7,
        out_specs=vmem,
        scratch_shapes=[
            pltpu.VMEM((tr // LANES * ch * tc if tr > LANES else 8, LANES), F32),
            pltpu.VMEM((ch * tr, tc), F32),
            pltpu.VMEM((q, nb, ch, bc * tc), BF),
            pltpu.VMEM((q * nb, ch, bc * tc), BF),
            pltpu.VMEM((nb, ch, lanes), BF),
            pltpu.VMEM((nb, ch, lanes), BF),
            pltpu.VMEM((nb, ch, lanes), BF),
            pltpu.VMEM((layers, hid, in_weight.shape[1]), BF),
            pltpu.VMEM((layers, hid, hid), BF),
            pltpu.VMEM((layers, hid, LANES), F32),
            pltpu.VMEM((layers, hid, LANES), F32),
            pltpu.VMEM((layers, ch, LANES), F32),
            pltpu.VMEM((bc, lanes), BF),
            pltpu.VMEM((lanes, width), BF),
            pltpu.VMEM((nb, 2 * ch, bc), BF),
            pltpu.VMEM((layers, ch, tr), F32),
            pltpu.VMEM((layers, ch, width), F32),
            pltpu.VMEM((layers, n_col - 1, ch, tr), F32),
            pltpu.VMEM((layers, n_row - 1, ch, width), F32),
            pltpu.VMEM((q, 2 * ch, width), BF),
            pltpu.VMEM((q, 2 * ch, width), BF),
            pltpu.VMEM((ch, tr), F32),
            pltpu.VMEM((ch, width), F32),
            dma((q, nb)),
            dma((q * nb,)),
            dma((layers, n_col - 1)),
            dma((layers, n_col - 1)),
            dma((layers, n_row - 1)),
            dma((layers, n_row - 1)),
            dma((q,)),
            dma((q,)),
        ],
        compiler_params=pltpu.CompilerParams(
            collective_id=0, has_side_effects=True, vmem_limit_bytes=60 * 1024 * 1024
        ),
    )(
        jnp.swapaxes(table, 1, 2).reshape(ch * tc, tr),
        in_weight,
        in_bias,
        mid_weight,
        mid_bias,
        jnp.swapaxes(out_weight, 1, 2),
        out_bias,
    )
    return jnp.swapaxes(result.reshape(ch, tc, tr), 1, 2)


def solution(mesh):
    placed = (P(None, "row", "col"), P(), P(), P(), P(), P(), P())
    return jax.shard_map(
        body, mesh=mesh, in_specs=placed, out_specs=P(None, "row", "col"), check_vma=False
    )
```

```python
import functools
import math

import jax
import jax.numpy as jnp
from jax import lax
from jax.experimental import pallas as pl
from jax.experimental.pallas import tpu as pltpu
from jax.sharding import PartitionSpec as P

MESH = pl.DeviceIdType.MESH
BF = jnp.bfloat16
F32 = jnp.float32
LANES = 128


def dot(a, b):
    return jnp.dot(a, b, preferred_element_type=F32)


def kernel(
    dims,
    table,
    w_in,
    b_in,
    w_mid,
    b_mid,
    w_out,
    b_out,
    out,
    flat,
    turned,
    send,
    pair,
    relay,
    own,
    own2,
    mir2,
    wt_in,
    wt_mid,
    bt_in,
    bt_mid,
    bt_out,
    spread,
    gather,
    col_chunks,
    row_part,
    col_part,
    row_recv,
    col_recv,
    mate_send,
    mate_recv,
    acc_row,
    acc_col,
    bulk_ssem,
    bulk_rsem,
    relay_ssem,
    relay_rsem,
    row_ssem,
    row_rsem,
    col_ssem,
    col_rsem,
    mate_ssem,
    mate_rsem,
):
    ch, tr, tc, n_row, n_col, q, nb, layers = dims
    pack = LANES // tc if tc < LANES else 1
    width = pack * tc
    bc = tc // nb
    lanes = bc * tr
    hid = w_mid.shape[1]
    scale = 1.0 / math.sqrt(tr * n_row)
    r = lax.axis_index("row")
    c = lax.axis_index("col")
    mir_r = c // q
    mir_c0 = q * r
    slot = c % q
    diag = mir_r == r

    barrier = pltpu.get_barrier_semaphore()
    for d in range(1, n_col):
        pl.semaphore_signal(
            barrier, inc=1, device_id=(r, lax.rem(c + d, n_col)), device_id_type=MESH
        )
    for d in range(1, n_row):
        pl.semaphore_signal(
            barrier, inc=1, device_id=(lax.rem(r + d, n_row), c), device_id_type=MESH
        )

    @pl.when(jnp.logical_not(diag))
    def _():
        for h in range(q):
            pl.semaphore_signal(
                barrier, inc=1, device_id=(mir_r, mir_c0 + h), device_id_type=MESH
            )

    groups = tr // LANES

    if groups > 1:
        for v in range(groups):
            flat[v * ch * tc : (v + 1) * ch * tc, :] = table[:, v * LANES : (v + 1) * LANES]

    def column_of(j):
        if groups == 1:
            return table[pl.ds(j, ch, stride=tc), :]
        parts = [flat[pl.ds(v * ch * tc + j, ch, stride=tc), :] for v in range(groups)]
        return jnp.concatenate(parts, axis=1)

    def turn_step(i, carry):
        src = pl.multiple_of(i * tc, tc)
        dst = pl.multiple_of(i * tr, tr)
        turned[pl.ds(dst, tr), :] = table[pl.ds(src, tc), :].T
        return carry

    lax.fori_loop(0, ch, turn_step, 0, unroll=4)

    def own_step(g, acc):
        for m in range(bc):
            val = column_of(g * bc + m)
            acc = acc + val
            own[g, :, m * tr : (m + 1) * tr] = val.astype(BF)
        return acc

    row_part[0] = lax.fori_loop(0, nb, own_step, jnp.zeros((ch, tr), F32))

    def col_step(i, acc):
        for u in range(8):
            acc = acc + turned[pl.ds(i * 8 + u, ch, stride=tr), :]
        return acc

    acc = lax.fori_loop(0, tr // 8, col_step, jnp.zeros((ch, tc), F32))
    col_part[0] = jnp.concatenate([acc] * pack, axis=1) if pack > 1 else acc

    @pl.when(diag)
    def _():
        pl.semaphore_wait(barrier, n_col - 1 + n_row - 1)

    @pl.when(jnp.logical_not(diag))
    def _():
        pl.semaphore_wait(barrier, n_col - 1 + n_row - 1 + q)

    def row_copy(layer, d):
        return pltpu.make_async_remote_copy(
            src_ref=row_part.at[layer],
            dst_ref=row_recv.at[layer, d - 1],
            send_sem=row_ssem.at[layer, d - 1],
            recv_sem=row_rsem.at[layer, d - 1],
            device_id=(r, lax.rem(c + d, n_col)),
            device_id_type=MESH,
        )

    def col_copy(layer, d):
        return pltpu.make_async_remote_copy(
            src_ref=col_part.at[layer],
            dst_ref=col_recv.at[layer, d - 1],
            send_sem=col_ssem.at[layer, d - 1],
            recv_sem=col_rsem.at[layer, d - 1],
            device_id=(lax.rem(r + d, n_row), c),
            device_id_type=MESH,
        )

    def pools_start(layer):
        for d in range(1, n_row):
            col_copy(layer, d).start()
        for d in range(1, n_col):
            row_copy(layer, d).start()

    def pools_finish(layer):
        row_sum = row_part[layer]
        col_sum = col_part[layer]
        for d in range(1, n_row):
            col_copy(layer, d).wait()
            col_sum = col_sum + col_recv[layer, d - 1]
        for d in range(1, n_col):
            row_copy(layer, d).wait()
            row_sum = row_sum + row_recv[layer, d - 1]
        return row_sum * scale, col_sum * scale

    pools_start(0)

    def bulk_copy(h, k):
        return pltpu.make_async_remote_copy(
            src_ref=send.at[h, k],
            dst_ref=pair.at[slot * nb + k],
            send_sem=bulk_ssem.at[h, k],
            recv_sem=bulk_rsem.at[slot * nb + k],
            device_id=(mir_r, mir_c0 + h),
            device_id_type=MESH,
        )

    def first_leg(h, k):
        d = lax.rem(mir_c0 + h - c + n_col, n_col)
        return pltpu.make_async_remote_copy(
            src_ref=send.at[h, k],
            dst_ref=relay.at[d - 1, k // 2],
            send_sem=bulk_ssem.at[h, k],
            recv_sem=relay_rsem.at[d - 1, k // 2],
            device_id=(r, mir_c0 + h),
            device_id_type=MESH,
        )

    def second_leg(d, m):
        start = lax.rem(c - d + n_col, n_col)
        at = lax.rem(start, q) * nb + 2 * m + 1
        return pltpu.make_async_remote_copy(
            src_ref=relay.at[d - 1, m],
            dst_ref=pair.at[at],
            send_sem=relay_ssem.at[d - 1, m],
            recv_sem=bulk_rsem.at[at],
            device_id=(start // q, c),
            device_id_type=MESH,
        )

    def relays(d):
        start = lax.rem(c - d + n_col, n_col)
        return jnp.logical_and(diag, start // q != r)

    def stay_copy(h, k):
        return pltpu.make_async_copy(
            send.at[h, k], pair.at[slot * nb + k], bulk_rsem.at[slot * nb + k]
        )

    for k in range(nb):
        for h in range(q):
            for m in range(bc // pack):
                base = h * tc + k * bc + m * pack
                parts = [turned[pl.ds(base + u, ch, stride=tr), :] for u in range(pack)]
                val = jnp.concatenate(parts, axis=1) if pack > 1 else parts[0]
                send[h, k, :, m * width : (m + 1) * width] = val.astype(BF)
        for h in range(q):
            here = jnp.logical_and(diag, slot == h)

            @pl.when(here)
            def _():
                stay_copy(h, k).start()

            direct = jnp.logical_not(here) if k % 2 == 0 else jnp.logical_and(diag, slot != h)

            @pl.when(direct)
            def _():
                bulk_copy(h, k).start()

            if k % 2 == 1:

                @pl.when(jnp.logical_not(diag))
                def _():
                    first_leg(h, k).start()

    for layer in range(layers):
        wt_in[layer] = w_in[layer].astype(F32).T.astype(BF)
        wt_mid[layer] = w_mid[layer].astype(F32).T.astype(BF)
        bt_in[layer] = jnp.broadcast_to(b_in[layer : layer + 1, :], (LANES, hid)).T
        bt_mid[layer] = jnp.broadcast_to(b_mid[layer : layer + 1, :], (LANES, hid)).T
        bt_out[layer] = jnp.broadcast_to(b_out[layer : layer + 1, :], (LANES, ch)).T
    cell_col = lax.broadcasted_iota(jnp.int32, (bc, lanes), 1) // tr
    spread[...] = jnp.where(
        cell_col == lax.broadcasted_iota(jnp.int32, (bc, lanes), 0), 1.0, 0.0
    ).astype(BF)
    cell_col = lax.broadcasted_iota(jnp.int32, (lanes, width), 0) // tr
    gather[...] = jnp.where(
        cell_col == lax.broadcasted_iota(jnp.int32, (lanes, width), 1), 1.0, 0.0
    ).astype(BF)

    rp, cp = pools_finish(0)
    rp = rp.astype(BF)
    cp = cp.astype(BF)
    for h in range(q):
        half = rp[:, h * tc : (h + 1) * tc]
        half = jnp.concatenate([half] * pack, axis=1) if pack > 1 else half
        mate_send[h, :ch, :] = half
        mate_send[h, ch:, :] = cp

    def mate_copy(h):
        return pltpu.make_async_remote_copy(
            src_ref=mate_send.at[h],
            dst_ref=mate_recv.at[slot],
            send_sem=mate_ssem.at[h],
            recv_sem=mate_rsem.at[slot],
            device_id=(mir_r, mir_c0 + h),
            device_id_type=MESH,
        )

    def mate_stay(h):
        return pltpu.make_async_copy(mate_send.at[h], mate_recv.at[slot], mate_rsem.at[slot])

    for h in range(q):
        here = jnp.logical_and(diag, slot == h)

        @pl.when(here)
        def _():
            mate_stay(h).start()

        @pl.when(jnp.logical_not(here))
        def _():
            mate_copy(h).start()

    for t in range(q):
        pltpu.make_async_copy(mate_send.at[0], mate_recv.at[t], mate_rsem.at[t]).wait()
    cp_rows = jnp.concatenate([mate_recv[t, ch:, :tc] for t in range(q)], axis=1)
    rp_rows = rp
    for g in range(nb):
        col_chunks[g, :ch, :] = cp[:, g * bc : (g + 1) * bc]
        col_chunks[g, ch:, :] = mate_recv[0, :ch, g * bc : (g + 1) * bc]

    def tile(x):
        return jnp.concatenate([x] * (lanes // x.shape[1]), axis=1)

    def network(layer, feats):
        h1 = dot(wt_in[layer], feats) + tile(bt_in[layer])
        h1 = jnp.maximum(h1, 0.0).astype(BF)
        h2 = dot(wt_mid[layer], h1) + tile(bt_mid[layer])
        h2 = jnp.maximum(h2, 0.0).astype(BF)
        return dot(w_out[layer], h2) + tile(bt_out[layer])

    acc_row[...] = jnp.zeros_like(acc_row)
    acc_col[...] = jnp.zeros_like(acc_col)

    def layer_one(g, carry):
        for d in range(1, n_col):

            @pl.when(jnp.logical_and(relays(d), g % 2 == 0))
            def _():
                pltpu.make_async_copy(
                    send.at[0, 0], relay.at[d - 1, g // 2], relay_rsem.at[d - 1, g // 2]
                ).wait()
                second_leg(d, g // 2).start()

        for t in range(q):
            pltpu.make_async_copy(
                send.at[0, 0], pair.at[t * nb + g], bulk_rsem.at[t * nb + g]
            ).wait()
        mine = own[g]
        pieces = [
            pair[t * nb + g, :, a * tc : (a + 1) * tc] for a in range(bc) for t in range(q)
        ]
        theirs = jnp.concatenate(pieces, axis=1)
        wide = dot(col_chunks[g], spread[...]).astype(BF)
        straight = jnp.concatenate([mine, theirs, tile(rp_rows), wide[:ch]], axis=0)
        value = network(0, straight)
        top = value.astype(BF)
        own2[g] = top
        low = (value - top.astype(F32)).astype(BF)
        sums = dot(jnp.concatenate([top, low], axis=0), gather[...])
        sums = sums[:ch] + sums[ch:]
        acc_col[...] += pltpu.roll(sums, g * bc, 1)
        total = acc_row[...]
        for m in range(bc):
            total = total + value[:, m * tr : (m + 1) * tr]
        acc_row[...] = total
        mirrored = jnp.concatenate([theirs, mine, wide[ch:], tile(cp_rows)], axis=0)
        mir2[g] = network(0, mirrored).astype(BF)
        return carry

    lax.fori_loop(0, nb, layer_one, 0)
    row_part[1] = acc_row[...]
    col_part[1] = acc_col[...]
    pools_start(1)

    for k in range(nb):
        for h in range(q):
            here = jnp.logical_and(diag, slot == h)

            @pl.when(jnp.logical_not(here))
            def _():
                bulk_copy(h, k).wait_send()

    for d in range(1, n_col):

        @pl.when(relays(d))
        def _():
            for m in range(nb // 2):
                second_leg(d, m).wait_send()

    for h in range(q):
        here = jnp.logical_and(diag, slot == h)

        @pl.when(jnp.logical_not(here))
        def _():
            mate_copy(h).wait_send()

    rp, cp = pools_finish(1)
    rp_two = rp.astype(BF)
    cp = cp.astype(BF)
    for g in range(nb):
        col_chunks[g, :ch, :] = cp[:, g * bc : (g + 1) * bc]

    def layer_two(g, carry):
        wide = dot(col_chunks[g, :ch, :], spread[...]).astype(BF)
        feats = jnp.concatenate([own2[g], mir2[g], tile(rp_two), wide], axis=0)
        value = network(1, feats)
        for m in range(bc):
            for v in range(groups):
                at = m * tr + v * LANES
                rows = pl.ds(v * ch * tc + g * bc + m, ch, stride=tc)
                if groups == 1:
                    out[rows, :] = value[:, at : at + LANES]
                else:
                    flat[rows, :] = value[:, at : at + LANES]
        return carry

    lax.fori_loop(0, nb, layer_two, 0)
    if groups > 1:
        for v in range(groups):
            out[:, v * LANES : (v + 1) * LANES] = flat[v * ch * tc : (v + 1) * ch * tc, :]


def body(table, in_weight, in_bias, mid_weight, mid_bias, out_weight, out_bias):
    ch, tr, tc = table.shape
    n_row = lax.axis_size("row")
    n_col = lax.axis_size("col")
    layers, _, hid = in_weight.shape
    q = tr // tc
    assert tr == q * tc and n_col == q * n_row
    nb = 8
    pack = LANES // tc if tc < LANES else 1
    width = pack * tc
    bc = tc // nb
    lanes = bc * tr
    dims = (ch, tr, tc, n_row, n_col, q, nb, layers)
    dma = pltpu.SemaphoreType.DMA
    vmem = pl.BlockSpec(memory_space=pltpu.VMEM)
    result = pl.pallas_call(
        functools.partial(kernel, dims),
        out_shape=jax.ShapeDtypeStruct((ch * tc, tr), F32),
        in_specs=[vmem] * 7,
        out_specs=vmem,
        scratch_shapes=[
            pltpu.VMEM((tr // LANES * ch * tc if tr > LANES else 8, LANES), F32),
            pltpu.VMEM((ch * tr, tc), F32),
            pltpu.VMEM((q, nb, ch, bc * tc), BF),
            pltpu.VMEM((q * nb, ch, bc * tc), BF),
            pltpu.VMEM((n_col - 1, nb // 2, ch, bc * tc), BF),
            pltpu.VMEM((nb, ch, lanes), BF),
            pltpu.VMEM((nb, ch, lanes), BF),
            pltpu.VMEM((nb, ch, lanes), BF),
            pltpu.VMEM((layers, hid, in_weight.shape[1]), BF),
            pltpu.VMEM((layers, hid, hid), BF),
            pltpu.VMEM((layers, hid, LANES), F32),
            pltpu.VMEM((layers, hid, LANES), F32),
            pltpu.VMEM((layers, ch, LANES), F32),
            pltpu.VMEM((bc, lanes), BF),
            pltpu.VMEM((lanes, width), BF),
            pltpu.VMEM((nb, 2 * ch, bc), BF),
            pltpu.VMEM((layers, ch, tr), F32),
            pltpu.VMEM((layers, ch, width), F32),
            pltpu.VMEM((layers, n_col - 1, ch, tr), F32),
            pltpu.VMEM((layers, n_row - 1, ch, width), F32),
            pltpu.VMEM((q, 2 * ch, width), BF),
            pltpu.VMEM((q, 2 * ch, width), BF),
            pltpu.VMEM((ch, tr), F32),
            pltpu.VMEM((ch, width), F32),
            dma((q, nb)),
            dma((q * nb,)),
            dma((n_col - 1, nb // 2)),
            dma((n_col - 1, nb // 2)),
            dma((layers, n_col - 1)),
            dma((layers, n_col - 1)),
            dma((layers, n_row - 1)),
            dma((layers, n_row - 1)),
            dma((q,)),
            dma((q,)),
        ],
        compiler_params=pltpu.CompilerParams(
            collective_id=0, has_side_effects=True, vmem_limit_bytes=60 * 1024 * 1024
        ),
    )(
        jnp.swapaxes(table, 1, 2).reshape(ch * tc, tr),
        in_weight,
        in_bias,
        mid_weight,
        mid_bias,
        jnp.swapaxes(out_weight, 1, 2),
        out_bias,
    )
    return jnp.swapaxes(result.reshape(ch, tc, tr), 1, 2)


def solution(mesh):
    placed = (P(None, "row", "col"), P(), P(), P(), P(), P(), P())
    return jax.shard_map(
        body, mesh=mesh, in_specs=placed, out_specs=P(None, "row", "col"), check_vma=False
    )
```

```python
import functools
import math

import jax
import jax.numpy as jnp
from jax import lax
from jax.experimental import pallas as pl
from jax.experimental.pallas import tpu as pltpu
from jax.sharding import PartitionSpec as P

MESH = pl.DeviceIdType.MESH
BF = jnp.bfloat16
F32 = jnp.float32
LANES = 128


def dot(a, b):
    return jnp.dot(a, b, preferred_element_type=F32)


def kernel(
    dims,
    table,
    w_in,
    b_in,
    w_mid,
    b_mid,
    w_out,
    b_out,
    out,
    flat,
    turned,
    send,
    pair,
    relay,
    own,
    own2,
    mir2,
    wt_in,
    wt_mid,
    bt_in,
    bt_mid,
    bt_out,
    spread,
    gather,
    col_chunks,
    row_part,
    col_part,
    row_recv,
    col_recv,
    mate_send,
    mate_recv,
    acc_row,
    acc_col,
    bulk_ssem,
    bulk_rsem,
    relay_ssem,
    relay_rsem,
    row_ssem,
    row_rsem,
    col_ssem,
    col_rsem,
    mate_ssem,
    mate_rsem,
):
    ch, tr, tc, n_row, n_col, q, nb, layers = dims
    pack = LANES // tc if tc < LANES else 1
    width = pack * tc
    bc = tc // nb
    lanes = bc * tr
    hid = w_mid.shape[1]
    scale = 1.0 / math.sqrt(tr * n_row)
    r = lax.axis_index("row")
    c = lax.axis_index("col")
    mir_r = c // q
    mir_c0 = q * r
    slot = c % q
    diag = mir_r == r

    barrier = pltpu.get_barrier_semaphore()
    for d in range(1, n_col):
        pl.semaphore_signal(
            barrier, inc=1, device_id=(r, lax.rem(c + d, n_col)), device_id_type=MESH
        )
    for d in range(1, n_row):
        pl.semaphore_signal(
            barrier, inc=1, device_id=(lax.rem(r + d, n_row), c), device_id_type=MESH
        )

    @pl.when(jnp.logical_not(diag))
    def _():
        for h in range(q):
            pl.semaphore_signal(
                barrier, inc=1, device_id=(mir_r, mir_c0 + h), device_id_type=MESH
            )

    groups = tr // LANES

    if groups > 1:
        for v in range(groups):
            flat[v * ch * tc : (v + 1) * ch * tc, :] = table[:, v * LANES : (v + 1) * LANES]

    def column_of(j):
        if groups == 1:
            return table[pl.ds(j, ch, stride=tc), :]
        parts = [flat[pl.ds(v * ch * tc + j, ch, stride=tc), :] for v in range(groups)]
        return jnp.concatenate(parts, axis=1)

    def turn_step(i, carry):
        src = pl.multiple_of(i * tc, tc)
        dst = pl.multiple_of(i * tr, tr)
        turned[pl.ds(dst, tr), :] = table[pl.ds(src, tc), :].T
        return carry

    lax.fori_loop(0, ch, turn_step, 0, unroll=4)

    def own_step(g, acc):
        for m in range(bc):
            val = column_of(g * bc + m)
            acc = acc + val
            own[g, :, m * tr : (m + 1) * tr] = val.astype(BF)
        return acc

    row_part[0] = lax.fori_loop(0, nb, own_step, jnp.zeros((ch, tr), F32))

    def col_step(i, acc):
        for u in range(8):
            acc = acc + turned[pl.ds(i * 8 + u, ch, stride=tr), :]
        return acc

    acc = lax.fori_loop(0, tr // 8, col_step, jnp.zeros((ch, tc), F32))
    col_part[0] = jnp.concatenate([acc] * pack, axis=1) if pack > 1 else acc

    @pl.when(diag)
    def _():
        pl.semaphore_wait(barrier, n_col - 1 + n_row - 1)

    @pl.when(jnp.logical_not(diag))
    def _():
        pl.semaphore_wait(barrier, n_col - 1 + n_row - 1 + q)

    def row_copy(layer, d):
        return pltpu.make_async_remote_copy(
            src_ref=row_part.at[layer],
            dst_ref=row_recv.at[layer, d - 1],
            send_sem=row_ssem.at[layer, d - 1],
            recv_sem=row_rsem.at[layer, d - 1],
            device_id=(r, lax.rem(c + d, n_col)),
            device_id_type=MESH,
        )

    def col_copy(layer, d):
        return pltpu.make_async_remote_copy(
            src_ref=col_part.at[layer],
            dst_ref=col_recv.at[layer, d - 1],
            send_sem=col_ssem.at[layer, d - 1],
            recv_sem=col_rsem.at[layer, d - 1],
            device_id=(lax.rem(r + d, n_row), c),
            device_id_type=MESH,
        )

    def pools_start(layer):
        for d in range(1, n_row):
            col_copy(layer, d).start()
        for d in range(1, n_col):
            row_copy(layer, d).start()

    def pools_finish(layer):
        row_sum = row_part[layer]
        col_sum = col_part[layer]
        for d in range(1, n_row):
            col_copy(layer, d).wait()
            col_sum = col_sum + col_recv[layer, d - 1]
        for d in range(1, n_col):
            row_copy(layer, d).wait()
            row_sum = row_sum + row_recv[layer, d - 1]
        return row_sum * scale, col_sum * scale

    pools_start(0)

    def bulk_copy(h, k):
        return pltpu.make_async_remote_copy(
            src_ref=send.at[h, k],
            dst_ref=pair.at[slot * nb + k],
            send_sem=bulk_ssem.at[h, k],
            recv_sem=bulk_rsem.at[slot * nb + k],
            device_id=(mir_r, mir_c0 + h),
            device_id_type=MESH,
        )

    def first_leg(h, k):
        d = lax.rem(mir_c0 + h - c + n_col, n_col)
        return pltpu.make_async_remote_copy(
            src_ref=send.at[h, k],
            dst_ref=relay.at[d - 1, k // 2],
            send_sem=bulk_ssem.at[h, k],
            recv_sem=relay_rsem.at[d - 1, k // 2],
            device_id=(r, mir_c0 + h),
            device_id_type=MESH,
        )

    def second_leg(d, m):
        start = lax.rem(c - d + n_col, n_col)
        at = lax.rem(start, q) * nb + 2 * m + 1
        return pltpu.make_async_remote_copy(
            src_ref=relay.at[d - 1, m],
            dst_ref=pair.at[at],
            send_sem=relay_ssem.at[d - 1, m],
            recv_sem=bulk_rsem.at[at],
            device_id=(start // q, c),
            device_id_type=MESH,
        )

    def relays(d):
        start = lax.rem(c - d + n_col, n_col)
        return jnp.logical_and(diag, start // q != r)

    def stay_copy(h, k):
        return pltpu.make_async_copy(
            send.at[h, k], pair.at[slot * nb + k], bulk_rsem.at[slot * nb + k]
        )

    for k in range(nb):
        for h in range(q):
            for m in range(bc // pack):
                base = h * tc + k * bc + m * pack
                parts = [turned[pl.ds(base + u, ch, stride=tr), :] for u in range(pack)]
                val = jnp.concatenate(parts, axis=1) if pack > 1 else parts[0]
                send[h, k, :, m * width : (m + 1) * width] = val.astype(BF)
        for h in range(q):
            here = jnp.logical_and(diag, slot == h)

            @pl.when(here)
            def _():
                stay_copy(h, k).start()

            direct = jnp.logical_not(here) if k % 2 == 0 else jnp.logical_and(diag, slot != h)

            @pl.when(direct)
            def _():
                bulk_copy(h, k).start()

            if k % 2 == 1:

                @pl.when(jnp.logical_not(diag))
                def _():
                    first_leg(h, k).start()

    for layer in range(layers):
        wt_in[layer] = w_in[layer].astype(F32).T.astype(BF)
        wt_mid[layer] = w_mid[layer].astype(F32).T.astype(BF)
        bt_in[layer] = jnp.broadcast_to(b_in[layer : layer + 1, :], (LANES, hid)).T
        bt_mid[layer] = jnp.broadcast_to(b_mid[layer : layer + 1, :], (LANES, hid)).T
        bt_out[layer] = jnp.broadcast_to(b_out[layer : layer + 1, :], (LANES, ch)).T
    cell_col = lax.broadcasted_iota(jnp.int32, (bc, lanes), 1) // tr
    spread[...] = jnp.where(
        cell_col == lax.broadcasted_iota(jnp.int32, (bc, lanes), 0), 1.0, 0.0
    ).astype(BF)
    cell_col = lax.broadcasted_iota(jnp.int32, (lanes, width), 0) // tr
    gather[...] = jnp.where(
        cell_col == lax.broadcasted_iota(jnp.int32, (lanes, width), 1), 1.0, 0.0
    ).astype(BF)

    rp, cp = pools_finish(0)
    rp = rp.astype(BF)
    cp = cp.astype(BF)
    for h in range(q):
        half = rp[:, h * tc : (h + 1) * tc]
        half = jnp.concatenate([half] * pack, axis=1) if pack > 1 else half
        mate_send[h, :ch, :] = half
        mate_send[h, ch:, :] = cp

    def mate_copy(h):
        return pltpu.make_async_remote_copy(
            src_ref=mate_send.at[h],
            dst_ref=mate_recv.at[slot],
            send_sem=mate_ssem.at[h],
            recv_sem=mate_rsem.at[slot],
            device_id=(mir_r, mir_c0 + h),
            device_id_type=MESH,
        )

    def mate_stay(h):
        return pltpu.make_async_copy(mate_send.at[h], mate_recv.at[slot], mate_rsem.at[slot])

    for h in range(q):
        here = jnp.logical_and(diag, slot == h)

        @pl.when(here)
        def _():
            mate_stay(h).start()

        @pl.when(jnp.logical_not(here))
        def _():
            mate_copy(h).start()

    for t in range(q):
        pltpu.make_async_copy(mate_send.at[0], mate_recv.at[t], mate_rsem.at[t]).wait()
    cp_rows = jnp.concatenate([mate_recv[t, ch:, :tc] for t in range(q)], axis=1)
    rp_rows = rp
    for g in range(nb):
        col_chunks[g, :ch, :] = cp[:, g * bc : (g + 1) * bc]
        col_chunks[g, ch:, :] = mate_recv[0, :ch, g * bc : (g + 1) * bc]

    def tile(x):
        return jnp.concatenate([x] * (lanes // x.shape[1]), axis=1)

    def network(layer, feats):
        h1 = dot(wt_in[layer], feats) + tile(bt_in[layer])
        h1 = jnp.maximum(h1, 0.0).astype(BF)
        h2 = dot(wt_mid[layer], h1) + tile(bt_mid[layer])
        h2 = jnp.maximum(h2, 0.0).astype(BF)
        return dot(w_out[layer], h2) + tile(bt_out[layer])

    acc_row[...] = jnp.zeros_like(acc_row)
    acc_col[...] = jnp.zeros_like(acc_col)

    late = nb // 2 - 1

    def mirror_one(g, carry):
        wide = dot(col_chunks[g, ch:, :], spread[...]).astype(BF)
        mirrored = jnp.concatenate([mir2[g], own[g], wide, tile(cp_rows)], axis=0)
        mir2[g] = network(0, mirrored).astype(BF)
        return carry

    def layer_one(g, carry):
        for d in range(1, n_col):

            @pl.when(jnp.logical_and(relays(d), g % 2 == 0))
            def _():
                pltpu.make_async_copy(
                    send.at[0, 0], relay.at[d - 1, g // 2], relay_rsem.at[d - 1, g // 2]
                ).wait()
                second_leg(d, g // 2).start()

        for t in range(q):
            pltpu.make_async_copy(
                send.at[0, 0], pair.at[t * nb + g], bulk_rsem.at[t * nb + g]
            ).wait()
        mine = own[g]
        pieces = [
            pair[t * nb + g, :, a * tc : (a + 1) * tc] for a in range(bc) for t in range(q)
        ]
        theirs = jnp.concatenate(pieces, axis=1)
        mir2[g] = theirs
        wide = dot(col_chunks[g, :ch, :], spread[...]).astype(BF)
        straight = jnp.concatenate([mine, theirs, tile(rp_rows), wide], axis=0)
        value = network(0, straight)
        top = value.astype(BF)
        own2[g] = top
        low = (value - top.astype(F32)).astype(BF)
        sums = dot(jnp.concatenate([top, low], axis=0), gather[...])
        sums = sums[:ch] + sums[ch:]
        acc_col[...] += pltpu.roll(sums, g * bc, 1)
        total = acc_row[...]
        for m in range(bc):
            total = total + value[:, m * tr : (m + 1) * tr]
        acc_row[...] = total

        @pl.when(g < nb - late)
        def _():
            mirror_one(g, 0)

        return carry

    lax.fori_loop(0, nb, layer_one, 0)
    row_part[1] = acc_row[...]
    col_part[1] = acc_col[...]
    pools_start(1)

    lax.fori_loop(nb - late, nb, mirror_one, 0)

    for k in range(nb):
        for h in range(q):
            here = jnp.logical_and(diag, slot == h)

            @pl.when(jnp.logical_not(here))
            def _():
                bulk_copy(h, k).wait_send()

    for d in range(1, n_col):

        @pl.when(relays(d))
        def _():
            for m in range(nb // 2):
                second_leg(d, m).wait_send()

    for h in range(q):
        here = jnp.logical_and(diag, slot == h)

        @pl.when(jnp.logical_not(here))
        def _():
            mate_copy(h).wait_send()

    rp, cp = pools_finish(1)
    rp_two = rp.astype(BF)
    cp = cp.astype(BF)
    for g in range(nb):
        col_chunks[g, :ch, :] = cp[:, g * bc : (g + 1) * bc]

    def layer_two(g, carry):
        wide = dot(col_chunks[g, :ch, :], spread[...]).astype(BF)
        feats = jnp.concatenate([own2[g], mir2[g], tile(rp_two), wide], axis=0)
        value = network(1, feats)
        for m in range(bc):
            for v in range(groups):
                at = m * tr + v * LANES
                rows = pl.ds(v * ch * tc + g * bc + m, ch, stride=tc)
                if groups == 1:
                    out[rows, :] = value[:, at : at + LANES]
                else:
                    flat[rows, :] = value[:, at : at + LANES]
        return carry

    lax.fori_loop(0, nb, layer_two, 0)
    if groups > 1:
        for v in range(groups):
            out[:, v * LANES : (v + 1) * LANES] = flat[v * ch * tc : (v + 1) * ch * tc, :]


def body(table, in_weight, in_bias, mid_weight, mid_bias, out_weight, out_bias):
    ch, tr, tc = table.shape
    n_row = lax.axis_size("row")
    n_col = lax.axis_size("col")
    layers, _, hid = in_weight.shape
    q = tr // tc
    assert tr == q * tc and n_col == q * n_row
    nb = 8
    pack = LANES // tc if tc < LANES else 1
    width = pack * tc
    bc = tc // nb
    lanes = bc * tr
    dims = (ch, tr, tc, n_row, n_col, q, nb, layers)
    dma = pltpu.SemaphoreType.DMA
    vmem = pl.BlockSpec(memory_space=pltpu.VMEM)
    result = pl.pallas_call(
        functools.partial(kernel, dims),
        out_shape=jax.ShapeDtypeStruct((ch * tc, tr), F32),
        in_specs=[vmem] * 7,
        out_specs=vmem,
        scratch_shapes=[
            pltpu.VMEM((tr // LANES * ch * tc if tr > LANES else 8, LANES), F32),
            pltpu.VMEM((ch * tr, tc), F32),
            pltpu.VMEM((q, nb, ch, bc * tc), BF),
            pltpu.VMEM((q * nb, ch, bc * tc), BF),
            pltpu.VMEM((n_col - 1, nb // 2, ch, bc * tc), BF),
            pltpu.VMEM((nb, ch, lanes), BF),
            pltpu.VMEM((nb, ch, lanes), BF),
            pltpu.VMEM((nb, ch, lanes), BF),
            pltpu.VMEM((layers, hid, in_weight.shape[1]), BF),
            pltpu.VMEM((layers, hid, hid), BF),
            pltpu.VMEM((layers, hid, LANES), F32),
            pltpu.VMEM((layers, hid, LANES), F32),
            pltpu.VMEM((layers, ch, LANES), F32),
            pltpu.VMEM((bc, lanes), BF),
            pltpu.VMEM((lanes, width), BF),
            pltpu.VMEM((nb, 2 * ch, bc), BF),
            pltpu.VMEM((layers, ch, tr), F32),
            pltpu.VMEM((layers, ch, width), F32),
            pltpu.VMEM((layers, n_col - 1, ch, tr), F32),
            pltpu.VMEM((layers, n_row - 1, ch, width), F32),
            pltpu.VMEM((q, 2 * ch, width), BF),
            pltpu.VMEM((q, 2 * ch, width), BF),
            pltpu.VMEM((ch, tr), F32),
            pltpu.VMEM((ch, width), F32),
            dma((q, nb)),
            dma((q * nb,)),
            dma((n_col - 1, nb // 2)),
            dma((n_col - 1, nb // 2)),
            dma((layers, n_col - 1)),
            dma((layers, n_col - 1)),
            dma((layers, n_row - 1)),
            dma((layers, n_row - 1)),
            dma((q,)),
            dma((q,)),
        ],
        compiler_params=pltpu.CompilerParams(
            collective_id=0, has_side_effects=True, vmem_limit_bytes=60 * 1024 * 1024
        ),
    )(
        jnp.swapaxes(table, 1, 2).reshape(ch * tc, tr),
        in_weight,
        in_bias,
        mid_weight,
        mid_bias,
        jnp.swapaxes(out_weight, 1, 2),
        out_bias,
    )
    return jnp.swapaxes(result.reshape(ch, tc, tr), 1, 2)


def solution(mesh):
    placed = (P(None, "row", "col"), P(), P(), P(), P(), P(), P())
    return jax.shard_map(
        body, mesh=mesh, in_specs=placed, out_specs=P(None, "row", "col"), check_vma=False
    )
```
